32 devices in a mesh: aa: 8 (over z, x), ba: 4 (over y, core).
Axes of the slice: x: 2, y: 2, z: 4, core: 2. Of those that a mesh axis runs over, the one named last changes fastest.
Arguments:
- patches: bfloat16 [8, 64, 512], P('ba'), may hold values from -6 to 6
- token_first: bfloat16 [8, 64, 256], P('aa'), may hold values from -0.75 to 0.75
- token_second: bfloat16 [8, 64, 256], P('aa'), may hold values from -0.375 to 0.375
- channel_first: bfloat16 [8, 512, 2048], P('aa'), may hold values from -0.25 to 0.25
- channel_second: bfloat16 [8, 2048, 512], P('aa'), may hold values from -0.1875 to 0.1875
- gains: float32 [8, 2, 512], P('aa'), may hold values from 0.25 to 1.75
- final_gain: float32 [512], replicated, may hold values from 0.25 to 1.75
- head_weight: bfloat16 [512, 1000], replicated, may hold values from -2 to 2
- depths: int32 [16, 2], replicated, may hold values from 1 to 4
- widths: int32 [16, 8], replicated, may hold values from 1 to 4
- labels: int32 [8], P('ba'), may hold values from 0 to 999
Outputs:
- losses: float32 [16], replicated
The draws below stay inside these ranges and needn't reach their ends.
All inputs are finite; a program needn't handle non-finite values.
Results may differ from the reference program's by a relative error of at most 0.0012.
Values may be sent and summed in bfloat16 or wider, within the bound.
A program may use at most 64 MiB of HBM per device.

```python
import jax
import jax.numpy as jnp
from jax import lax

D = 512
DS = 256
DC = 2048
CLASSES = 1000
S = 64
UNIT = 4
CAND = 16
SECTIONS = 8
UNITS = 2
IMAGES = 8
N_AA = 8


def place_ends(result, stream_key, least, largest):
    index_at = [jax.random.randint(jax.random.fold_in(stream_key, axis), (), 0, length) for axis, length in enumerate(result.shape)]
    main_axis = result.shape.index(max(result.shape))
    beside = index_at[:main_axis] + [(index_at[main_axis] + 1) % result.shape[main_axis]] + index_at[main_axis + 1:]
    return result.at[tuple(index_at)].set(least).at[tuple(beside)].set(largest)


def block_scale(key, shape, split, least, top_value):
    def one(position, shards_of):
        heights = jax.random.uniform(jax.random.fold_in(jax.random.fold_in(key, 6), position), (shards_of,), jnp.float32, least / len(split), top_value / len(split))
        return jnp.repeat(jnp.exp(heights), shape[position] // shards_of).reshape((-1,) + (1,) * (len(shape) - position - 1))

    level = one(*split[0])
    for cut in split[1:]:
        level = level * one(*cut)
    return level


def scatter_about(stream_key, dims, deviation, bound, cuts=(), dtype=jnp.bfloat16):
    entries = deviation * jax.random.normal(stream_key, dims, jnp.float32)
    if cuts:
        entries = entries * block_scale(stream_key, dims, cuts, -0.22, 0.18)
    return jnp.clip(entries, -bound, bound).astype(dtype)


def setup_inputs(seed: int = 0) -> dict:
    streams_of = jax.random.split(jax.random.key(seed), 12)
    patches = scatter_about(streams_of[0], (IMAGES, S, D), 1.0, 6.0, ((0, 4),))
    token_first = scatter_about(streams_of[1], (SECTIONS, S, DS), S ** -0.5, 0.75, ((0, 8),))
    token_second = scatter_about(streams_of[2], (SECTIONS, S, DS), DS ** -0.5, 0.375, ((0, 8),))
    channel_first = scatter_about(streams_of[3], (SECTIONS, D, DC), D ** -0.5, 0.25, ((0, 8),))
    channel_second = scatter_about(streams_of[4], (SECTIONS, DC, D), (DC // 2) ** -0.5, 0.1875, ((0, 8),))
    gains = jnp.clip(1.0 + 0.15 * jax.random.normal(streams_of[5], (SECTIONS, 2, D), jnp.float32), 0.25, 1.75)
    final_gain = jnp.clip(1.0 + 0.15 * jax.random.normal(streams_of[6], (D,), jnp.float32), 0.25, 1.75)
    head_weight = scatter_about(streams_of[7], (D, CLASSES), (max(D // 64, 1)) ** -0.5, 2.0)
    depths = place_ends(jax.random.randint(streams_of[8], (CAND, UNITS), 1, 5), jax.random.fold_in(streams_of[8], 1), 1, 4).astype(jnp.int32)
    widths = place_ends(jax.random.randint(streams_of[9], (CAND, SECTIONS), 1, 5), jax.random.fold_in(streams_of[9], 1), 1, 4).astype(jnp.int32)
    labels = place_ends(jax.random.randint(streams_of[10], (IMAGES,), 0, CLASSES), jax.random.fold_in(streams_of[10], 1), 0, CLASSES - 1).astype(jnp.int32)
    return dict(patches=patches, token_first=token_first, token_second=token_second, channel_first=channel_first, channel_second=channel_second, gains=gains, final_gain=final_gain, head_weight=head_weight, depths=depths, widths=widths, labels=labels)


def layer_norm(values, gain):
    center = values - lax.optimization_barrier(jnp.mean(values, axis=-1, keepdims=True))
    spread = lax.optimization_barrier(jnp.mean(center * center, axis=-1, keepdims=True))
    return center * lax.rsqrt(spread + 1e-06) * gain

def mixer_block(state, token_first_weight, token_second_weight, channel_one, channel_two, gain_pair, width):
    floats = state.astype(jnp.float32)
    normalized_input = layer_norm(floats, gain_pair[0]).astype(jnp.bfloat16)
    token_before_mixing = jnp.einsum('gtc,tp->gpc', normalized_input.astype(jnp.float32), token_first_weight.astype(jnp.float32))
    token_mixing_hidden = jax.nn.gelu(token_before_mixing, approximate=True).astype(jnp.bfloat16)
    token_portion = jnp.einsum('hcx,mc->hmx', token_mixing_hidden.astype(jnp.float32), token_second_weight.astype(jnp.float32))
    mixed = floats + token_portion
    second = layer_norm(mixed, gain_pair[1]).astype(jnp.bfloat16)
    rows = second.reshape(-1, D)
    channel_pre = jnp.dot(rows, channel_one, preferred_element_type=jnp.float32)
    lanes = jnp.arange(DC).astype(jnp.int32)
    keep = lanes < width * (DC // 4)
    channel_hidden = jnp.where(keep[None, :], jax.nn.gelu(channel_pre, approximate=True), 0.0).astype(jnp.bfloat16)
    channel_portion = jnp.dot(channel_hidden, channel_two, preferred_element_type=jnp.float32)
    return (mixed + channel_portion.reshape(mixed.shape)).astype(jnp.bfloat16)

def head_loss(state, final_gain, head_weight, labels):
    normalized_input = layer_norm(state.astype(jnp.float32), final_gain)
    pooled = lax.optimization_barrier(jnp.mean(normalized_input, axis=1)).astype(jnp.bfloat16)
    logits = jnp.dot(pooled, head_weight, preferred_element_type=jnp.float32)
    total = jax.nn.logsumexp(logits, axis=-1)
    classes = jnp.arange(CLASSES).astype(jnp.int32)
    picked = lax.optimization_barrier(jnp.sum(jnp.where(classes[None, :] == labels[:, None], logits, 0.0), axis=-1))
    return jnp.sum(total - picked)

def reference(patches, token_first, token_second, channel_first, channel_second, gains, final_gain, head_weight, depths, widths, labels):

    def one_candidate(pair):
        depth_choice_row, width_row = pair
        state = patches
        for section in range(N_AA):
            updated = mixer_block(state, token_first[section], token_second[section], channel_first[section], channel_second[section], gains[section], width_row[section])
            active = section % UNIT < depth_choice_row[section // UNIT]
            state = jnp.where(active, updated, state)
        return head_loss(state, final_gain, head_weight, labels)
    return lax.map(one_candidate, (depths, widths))
```

```python
import functools

import jax
import jax.numpy as jnp
from jax import lax
from jax.experimental import pallas as pl
from jax.experimental.pallas import tpu as pltpu
from jax.sharding import PartitionSpec as P

UNIT = 4
QUARTERS = 4
MESH = pl.DeviceIdType.MESH
GELU_A = 0.7978845608028654
GELU_B = 0.044715 * GELU_A


def layer_norm(values, gain):
    center = values - jnp.mean(values, axis=-1, keepdims=True)
    spread = jnp.mean(center * center, axis=-1, keepdims=True)
    return center * lax.rsqrt(spread + 1e-06) * gain


def gelu(x, half):
    bent = jnp.tanh(x * (GELU_A + GELU_B * (x * x)))
    scaled = x * half
    return scaled + scaled * bent


def dot(a, b):
    return jnp.dot(a, b, preferred_element_type=jnp.float32)


def kernel(
    sections,
    shards,
    depths,
    widths,
    labels,
    patches,
    token_first,
    token_second,
    channel_first,
    channel_second,
    gains,
    final_gain,
    head_weight,
    out,
    inbox,
    outbox,
    token_first_t,
    pooled,
    share,
    landing,
    send_sem,
    recv_sem,
    share_sem,
    landing_sem,
):
    section = lax.axis_index("aa")
    shard = lax.axis_index("ba")
    last = sections - 1
    images, _, width_model = patches.shape
    candidates = depths.shape[0]
    units = candidates * images
    hidden_units = channel_first.shape[2]
    quarter = hidden_units // QUARTERS

    barrier = pltpu.get_barrier_semaphore()

    def greet(aa, ba):
        pl.semaphore_signal(barrier, inc=1, device_id=(aa, ba), device_id_type=MESH)

    @pl.when(section > 0)
    def _():
        greet(section - 1, shard)

    for other in range(shards):

        @pl.when(jnp.logical_or(section < last, shard != other))
        def _():
            greet(last, other)

    @pl.when(section < last)
    def _():
        pl.semaphore_wait(barrier, 1)

    @pl.when(section == last)
    def _():
        pl.semaphore_wait(barrier, sections * shards - 1)

    token_first_t[...] = token_first[0].T

    def hop(unit):
        return pltpu.make_async_remote_copy(
            src_ref=outbox.at[unit],
            dst_ref=inbox.at[unit],
            send_sem=send_sem.at[unit],
            recv_sem=recv_sem.at[unit],
            device_id=(lax.rem(section + 1, sections), shard),
            device_id_type=MESH,
        )

    def step(unit, carry):
        candidate = unit // images
        image = unit % images

        @pl.when(section == 0)
        def _():
            inbox[unit] = patches[image]

        @pl.when(section > 0)
        def _():
            hop(unit).wait_recv()

        width = widths[candidate, section]
        active = section % UNIT < depths[candidate, section // UNIT]
        state = inbox[unit]
        floats = state.astype(jnp.float32)
        normed = layer_norm(floats, gains[0, 0:1, :]).astype(jnp.bfloat16)
        token_hidden = gelu(dot(token_first_t[...], normed), 0.5).astype(jnp.bfloat16)
        mixed = floats + dot(token_second[0], token_hidden)
        second = layer_norm(mixed, gains[0, 1:2, :]).astype(jnp.bfloat16)
        total = mixed
        for index in range(QUARTERS):
            span = slice(index * quarter, (index + 1) * quarter)
            half = jnp.where(index < width, 0.5, 0.0)
            hidden = gelu(dot(second, channel_first[0, :, span]), half)
            total = total + dot(hidden.astype(jnp.bfloat16), channel_second[0, span, :])
        updated = jnp.where(active, total.astype(jnp.bfloat16), state)
        outbox[unit] = updated

        @pl.when(section < last)
        def _():
            hop(unit).start()

        @pl.when(section == last)
        def _():
            final = layer_norm(outbox[unit].astype(jnp.float32), final_gain[...])
            row = image * candidates + candidate
            pooled[pl.ds(row, 1), :] = jnp.mean(final, axis=0, keepdims=True)

        return carry

    lax.fori_loop(0, units, step, 0)

    def tell(aa, ba):
        return pltpu.make_async_remote_copy(
            src_ref=share,
            dst_ref=landing.at[shard],
            send_sem=share_sem.at[aa * shards + ba],
            recv_sem=landing_sem.at[shard],
            device_id=(aa, ba),
            device_id_type=MESH,
        )

    def each_other(act):
        def visit(target, carry):
            aa, ba = target // shards, target % shards

            @pl.when(jnp.logical_or(aa != section, ba != shard))
            def _():
                act(tell(aa, ba))

            return carry

        lax.fori_loop(0, sections * shards, visit, 0)

    @pl.when(section == last)
    def _():
        logits = dot(pooled[...].astype(jnp.bfloat16), head_weight[...])
        top = jnp.max(logits, axis=-1, keepdims=True)
        total = top + jnp.log(jnp.sum(jnp.exp(logits - top), axis=-1, keepdims=True))
        rows = lax.broadcasted_iota(jnp.int32, logits.shape, 0)
        classes = lax.broadcasted_iota(jnp.int32, logits.shape, 1)
        wanted = jnp.full(logits.shape, labels[0], jnp.int32)
        for image in range(1, images):
            wanted = jnp.where(rows >= image * candidates, labels[image], wanted)
        picked = jnp.sum(
            jnp.where(classes == wanted, logits, 0.0), axis=-1, keepdims=True
        )
        losses = total - picked
        summed = losses[:candidates]
        for image in range(1, images):
            summed = summed + losses[image * candidates : (image + 1) * candidates]
        lanes = out.shape[1]
        rows = lax.broadcasted_iota(jnp.int32, (candidates, lanes), 0)
        cols = lax.broadcasted_iota(jnp.int32, (candidates, lanes), 1)
        spread = jnp.broadcast_to(summed, (candidates, lanes))
        line = jnp.sum(jnp.where(rows == cols, spread, 0.0), axis=0, keepdims=True)
        share[...] = line
        landing[shard] = line
        each_other(lambda copy: copy.start())
        each_other(lambda copy: copy.wait_send())

    @pl.when(section < last)
    def _():
        def drain(unit, carry):
            hop(unit).wait_send()
            return carry

        lax.fori_loop(0, units, drain, 0)

    for origin in range(shards):

        @pl.when(jnp.logical_or(section < last, shard != origin))
        def _():
            pltpu.make_async_remote_copy(
                src_ref=share,
                dst_ref=landing.at[origin],
                send_sem=share_sem.at[0],
                recv_sem=landing_sem.at[origin],
                device_id=(last, origin),
                device_id_type=MESH,
            ).wait_recv()

    result = landing[0]
    for origin in range(1, shards):
        result = result + landing[origin]
    out[...] = result


def solution(mesh):
    sections, shards = mesh.shape["aa"], mesh.shape["ba"]

    def local(
        patches,
        token_first,
        token_second,
        channel_first,
        channel_second,
        gains,
        final_gain,
        head_weight,
        depths,
        widths,
        labels,
    ):
        images, patch_count, model = patches.shape
        candidates = depths.shape[0]
        units = candidates * images
        lanes = pl.cdiv(candidates, 128) * 128
        smem = pl.BlockSpec(memory_space=pltpu.SMEM)
        vmem = pl.BlockSpec(memory_space=pltpu.VMEM)
        line = pl.pallas_call(
            functools.partial(kernel, sections, shards),
            out_shape=jax.ShapeDtypeStruct((1, lanes), jnp.float32),
            in_specs=[smem] * 3 + [vmem] * 8,
            out_specs=vmem,
            scratch_shapes=[
                pltpu.VMEM((units, patch_count, model), jnp.bfloat16),
                pltpu.VMEM((units, patch_count, model), jnp.bfloat16),
                pltpu.VMEM((token_first.shape[2], patch_count), jnp.bfloat16),
                pltpu.VMEM((units, model), jnp.float32),
                pltpu.VMEM((1, lanes), jnp.float32),
                pltpu.VMEM((shards, 1, lanes), jnp.float32),
                pltpu.SemaphoreType.DMA((units,)),
                pltpu.SemaphoreType.DMA((units,)),
                pltpu.SemaphoreType.DMA((sections * shards,)),
                pltpu.SemaphoreType.DMA((shards,)),
            ],
            compiler_params=pltpu.CompilerParams(
                collective_id=0, has_side_effects=True
            ),
        )(
            depths,
            widths,
            labels,
            patches,
            token_first,
            token_second,
            channel_first,
            channel_second,
            gains,
            final_gain[None, :],
            head_weight,
        )
        return line[0, :candidates]

    return jax.shard_map(
        local,
        mesh=mesh,
        in_specs=(
            P("ba", None, None),
            P("aa", None, None),
            P("aa", None, None),
            P("aa", None, None),
            P("aa", None, None),
            P("aa", None, None),
            P(),
            P(),
            P(),
            P(),
            P("ba"),
        ),
        out_specs=P(),
        check_vma=False,
    )
```

```python
import functools

import jax
import jax.numpy as jnp
from jax import lax
from jax.experimental import pallas as pl
from jax.experimental.pallas import tpu as pltpu
from jax.sharding import PartitionSpec as P

UNIT = 4
QUARTERS = 4
MESH = pl.DeviceIdType.MESH
GELU_A = 0.7978845608028654
GELU_B = 0.044715 * GELU_A


def layer_norm(values, gain):
    center = values - jnp.mean(values, axis=-1, keepdims=True)
    spread = jnp.mean(center * center, axis=-1, keepdims=True)
    return center * lax.rsqrt(spread + 1e-06) * gain


def gelu(x, half):
    bent = jnp.tanh(x * (GELU_A + GELU_B * (x * x)))
    scaled = x * half
    return scaled + scaled * bent


def dot(a, b):
    return jnp.dot(a, b, preferred_element_type=jnp.float32)


def kernel(
    sections,
    shards,
    depths,
    widths,
    labels,
    patches,
    token_first,
    token_second,
    channel_first,
    channel_second,
    gains,
    final_gain,
    head_weight_t,
    out,
    inbox,
    outbox,
    token_one,
    token_two,
    channel_one,
    channel_two,
    head,
    token_one_t,
    pooled,
    share,
    landing,
    send_sem,
    recv_sem,
    share_sem,
    landing_sem,
    load_sem,
):
    section = lax.axis_index("aa")
    shard = lax.axis_index("ba")
    last = sections - 1
    images, patch_count, model = patches.shape
    candidates = depths.shape[1]
    units = candidates * images
    hidden_units = channel_first.shape[2]
    quarter = hidden_units // QUARTERS

    loads = [
        pltpu.make_async_copy(source.at[0], target, load_sem.at[index])
        for index, (source, target) in enumerate(
            (
                (token_first, token_one),
                (token_second, token_two),
                (channel_first, channel_one),
                (channel_second, channel_two),
            )
        )
    ]
    head_load = pltpu.make_async_copy(head_weight_t, head, load_sem.at[4])
    for load in loads:
        load.start()

    @pl.when(section == last)
    def _():
        head_load.start()

    barrier = pltpu.get_barrier_semaphore()

    def greet(aa, ba):
        pl.semaphore_signal(barrier, inc=1, device_id=(aa, ba), device_id_type=MESH)

    @pl.when(section > 0)
    def _():
        greet(section - 1, shard)

    for other in range(shards):

        @pl.when(jnp.logical_or(section < last, shard != other))
        def _():
            greet(last, other)

    @pl.when(section < last)
    def _():
        pl.semaphore_wait(barrier, 1)

    @pl.when(section == last)
    def _():
        pl.semaphore_wait(barrier, sections * shards - 1)

    loads[0].wait()
    token_one_t[...] = token_one[...].T
    loads[1].wait()

    def hop(unit):
        return pltpu.make_async_remote_copy(
            src_ref=outbox.at[unit],
            dst_ref=inbox.at[unit],
            send_sem=send_sem.at[unit],
            recv_sem=recv_sem.at[unit],
            device_id=(lax.rem(section + 1, sections), shard),
            device_id_type=MESH,
        )

    lane_of_hidden = lax.broadcasted_iota(jnp.int32, (1, hidden_units), 1)

    def step(candidate, carry):
        first = candidate * images

        @pl.when(section == 0)
        def _():
            for image in range(images):
                inbox[first + image] = patches[image]

        @pl.when(section > 0)
        def _():
            for image in range(images):
                hop(first + image).wait_recv()

        active = section % UNIT < depths[section // UNIT, candidate]
        half = jnp.where(lane_of_hidden < widths[section, candidate] * quarter, 0.5, 0.0)
        states = [inbox[first + image] for image in range(images)]
        floats = [state.astype(jnp.float32) for state in states]
        normed = jnp.concatenate(
            [layer_norm(value, gains[0, 0:1, :]).astype(jnp.bfloat16) for value in floats],
            axis=1,
        )
        token_hidden = gelu(dot(token_one_t[...], normed), 0.5).astype(jnp.bfloat16)
        token_part = dot(token_two[...], token_hidden)
        mixed = jnp.concatenate(
            [
                floats[image] + token_part[:, image * model : (image + 1) * model]
                for image in range(images)
            ],
            axis=0,
        )
        second = layer_norm(mixed, gains[0, 1:2, :]).astype(jnp.bfloat16)

        @pl.when(candidate == 0)
        def _():
            loads[2].wait()
            loads[3].wait()

        hidden = gelu(dot(second, channel_one[...]), half).astype(jnp.bfloat16)
        total = (mixed + dot(hidden, channel_two[...])).astype(jnp.bfloat16)
        for image in range(images):
            rows = slice(image * patch_count, (image + 1) * patch_count)
            outbox[first + image] = jnp.where(active, total[rows], states[image])

        @pl.when(section < last)
        def _():
            for image in range(images):
                hop(first + image).start()

        @pl.when(section == last)
        def _():
            for image in range(images):
                final = layer_norm(
                    outbox[first + image].astype(jnp.float32), final_gain[...]
                )
                pooled[pl.ds(image * candidates + candidate, 1), :] = jnp.mean(
                    final, axis=0, keepdims=True
                )

        return carry

    lax.fori_loop(0, candidates, step, 0)

    def tell(aa, ba):
        return pltpu.make_async_remote_copy(
            src_ref=share,
            dst_ref=landing.at[shard],
            send_sem=share_sem.at[aa * shards + ba],
            recv_sem=landing_sem.at[shard],
            device_id=(aa, ba),
            device_id_type=MESH,
        )

    def each_other(act):
        def visit(target, carry):
            aa, ba = target // shards, target % shards

            @pl.when(jnp.logical_or(aa != section, ba != shard))
            def _():
                act(tell(aa, ba))

            return carry

        lax.fori_loop(0, sections * shards, visit, 0)

    @pl.when(section == last)
    def _():
        head_load.wait()
        logits = lax.dot_general(
            pooled[...].astype(jnp.bfloat16),
            head[...],
            (((1,), (1,)), ((), ())),
            preferred_element_type=jnp.float32,
        )
        top = jnp.max(logits, axis=-1, keepdims=True)
        total = top + jnp.log(jnp.sum(jnp.exp(logits - top), axis=-1, keepdims=True))
        rows = lax.broadcasted_iota(jnp.int32, logits.shape, 0)
        classes = lax.broadcasted_iota(jnp.int32, logits.shape, 1)
        wanted = jnp.full(logits.shape, labels[0], jnp.int32)
        for image in range(1, images):
            wanted = jnp.where(rows >= image * candidates, labels[image], wanted)
        picked = jnp.sum(
            jnp.where(classes == wanted, logits, 0.0), axis=-1, keepdims=True
        )
        losses = total - picked
        summed = losses[:candidates]
        for image in range(1, images):
            summed = summed + losses[image * candidates : (image + 1) * candidates]
        lanes = out.shape[1]
        rows = lax.broadcasted_iota(jnp.int32, (candidates, lanes), 0)
        cols = lax.broadcasted_iota(jnp.int32, (candidates, lanes), 1)
        spread = jnp.broadcast_to(summed, (candidates, lanes))
        line = jnp.sum(jnp.where(rows == cols, spread, 0.0), axis=0, keepdims=True)
        share[...] = line
        landing[shard] = line
        each_other(lambda copy: copy.start())
        each_other(lambda copy: copy.wait_send())

    @pl.when(section < last)
    def _():
        def drain(unit, carry):
            hop(unit).wait_send()
            return carry

        lax.fori_loop(0, units, drain, 0)

    for origin in range(shards):

        @pl.when(jnp.logical_or(section < last, shard != origin))
        def _():
            pltpu.make_async_remote_copy(
                src_ref=share,
                dst_ref=landing.at[origin],
                send_sem=share_sem.at[0],
                recv_sem=landing_sem.at[origin],
                device_id=(last, origin),
                device_id_type=MESH,
            ).wait_recv()

    result = landing[0]
    for origin in range(1, shards):
        result = result + landing[origin]
    out[...] = result


def solution(mesh):
    sections, shards = mesh.shape["aa"], mesh.shape["ba"]

    def local(
        patches,
        token_first,
        token_second,
        channel_first,
        channel_second,
        gains,
        final_gain,
        head_weight,
        depths,
        widths,
        labels,
    ):
        images, patch_count, model = patches.shape
        candidates = depths.shape[0]
        units = candidates * images
        lanes = pl.cdiv(candidates, 128) * 128
        smem = pl.BlockSpec(memory_space=pltpu.SMEM)
        vmem = pl.BlockSpec(memory_space=pltpu.VMEM)
        hbm = pl.BlockSpec(memory_space=pl.ANY)
        line = pl.pallas_call(
            functools.partial(kernel, sections, shards),
            out_shape=jax.ShapeDtypeStruct((1, lanes), jnp.float32),
            in_specs=[smem] * 3 + [vmem] + [hbm] * 4 + [vmem] * 2 + [hbm],
            out_specs=vmem,
            scratch_shapes=[
                pltpu.VMEM((units, patch_count, model), jnp.bfloat16),
                pltpu.VMEM((units, patch_count, model), jnp.bfloat16),
                pltpu.VMEM(token_first.shape[1:], jnp.bfloat16),
                pltpu.VMEM(token_second.shape[1:], jnp.bfloat16),
                pltpu.VMEM(channel_first.shape[1:], jnp.bfloat16),
                pltpu.VMEM(channel_second.shape[1:], jnp.bfloat16),
                pltpu.VMEM(head_weight.shape[::-1], jnp.bfloat16),
                pltpu.VMEM((token_first.shape[2], patch_count), jnp.bfloat16),
                pltpu.VMEM((units, model), jnp.float32),
                pltpu.VMEM((1, lanes), jnp.float32),
                pltpu.VMEM((shards, 1, lanes), jnp.float32),
                pltpu.SemaphoreType.DMA((units,)),
                pltpu.SemaphoreType.DMA((units,)),
                pltpu.SemaphoreType.DMA((sections * shards,)),
                pltpu.SemaphoreType.DMA((shards,)),
                pltpu.SemaphoreType.DMA((5,)),
            ],
            compiler_params=pltpu.CompilerParams(
                collective_id=0, has_side_effects=True
            ),
        )(
            depths.T,
            widths.T,
            labels,
            patches,
            token_first,
            token_second,
            channel_first,
            channel_second,
            gains,
            final_gain[None, :],
            head_weight.T,
        )
        return line[0, :candidates]

    return jax.shard_map(
        local,
        mesh=mesh,
        in_specs=(
            P("ba", None, None),
            P("aa", None, None),
            P("aa", None, None),
            P("aa", None, None),
            P("aa", None, None),
            P("aa", None, None),
            P(),
            P(),
            P(),
            P(),
            P("ba"),
        ),
        out_specs=P(),
        check_vma=False,
    )
```

```python
import functools

import jax
import jax.numpy as jnp
from jax import lax
from jax.experimental import pallas as pl
from jax.experimental.pallas import tpu as pltpu
from jax.sharding import PartitionSpec as P

UNIT = 4
QUARTERS = 4
MESH = pl.DeviceIdType.MESH
GELU_A = 0.7978845608028654
GELU_B = 0.044715 * GELU_A


def layer_norm(values, gain):
    center = values - jnp.mean(values, axis=-1, keepdims=True)
    spread = jnp.mean(center * center, axis=-1, keepdims=True)
    return center * lax.rsqrt(spread + 1e-06) * gain


def gelu(x, half):
    bent = jnp.tanh(x * (GELU_A + GELU_B * (x * x)))
    scaled = x * half
    return scaled + scaled * bent


def dot(a, b):
    return jnp.dot(a, b, preferred_element_type=jnp.float32)


def kernel(
    sections,
    shards,
    depths,
    widths,
    labels,
    patches,
    token_first,
    token_second,
    channel_first,
    channel_second,
    gains,
    final_gain,
    head_weight_t,
    out,
    inbox,
    outbox,
    token_one,
    token_two,
    channel_one,
    channel_two,
    head,
    token_one_t,
    pooled,
    share,
    landing,
    send_sem,
    recv_sem,
    share_sem,
    landing_sem,
    load_sem,
):
    section = lax.axis_index("aa")
    shard = lax.axis_index("ba")
    last = sections - 1
    images, patch_count, model = patches.shape
    candidates = depths.shape[1]
    units = candidates * images
    hidden_units = channel_first.shape[2]
    quarter = hidden_units // QUARTERS

    loads = [
        pltpu.make_async_copy(source.at[0], target, load_sem.at[index])
        for index, (source, target) in enumerate(
            (
                (token_first, token_one),
                (token_second, token_two),
                (channel_first, channel_one),
                (channel_second, channel_two),
            )
        )
    ]
    head_load = pltpu.make_async_copy(head_weight_t, head, load_sem.at[4])
    for load in loads:
        load.start()

    @pl.when(section == last)
    def _():
        head_load.start()

    barrier = pltpu.get_barrier_semaphore()

    def greet(aa, ba):
        pl.semaphore_signal(barrier, inc=1, device_id=(aa, ba), device_id_type=MESH)

    @pl.when(section > 0)
    def _():
        greet(section - 1, shard)

    for other in range(shards):

        @pl.when(jnp.logical_or(section < last, shard != other))
        def _():
            greet(last, other)

    @pl.when(section < last)
    def _():
        pl.semaphore_wait(barrier, 1)

    @pl.when(section == last)
    def _():
        pl.semaphore_wait(barrier, sections * shards - 1)

    loads[0].wait()
    token_one_t[...] = token_one[...].T
    loads[1].wait()

    def hop(unit):
        return pltpu.make_async_remote_copy(
            src_ref=outbox.at[unit],
            dst_ref=inbox.at[unit],
            send_sem=send_sem.at[unit],
            recv_sem=recv_sem.at[unit],
            device_id=(lax.rem(section + 1, sections), shard),
            device_id_type=MESH,
        )

    lane_of_hidden = lax.broadcasted_iota(jnp.int32, (1, hidden_units), 1)

    def step(group, finish, index, carry):
        first = index * group
        candidate = first // images

        if finish:
            for image in range(group):
                hop(first + image).wait_recv()
        else:

            @pl.when(section == 0)
            def _():
                for image in range(group):
                    inbox[first + image] = patches[(first + image) % images]

            @pl.when(section > 0)
            def _():
                for image in range(group):
                    hop(first + image).wait_recv()

        active = section % UNIT < depths[section // UNIT, candidate]
        half = jnp.where(lane_of_hidden < widths[section, candidate] * quarter, 0.5, 0.0)
        states = [inbox[first + image] for image in range(group)]
        floats = [state.astype(jnp.float32) for state in states]
        normed = jnp.concatenate(
            [layer_norm(value, gains[0, 0:1, :]).astype(jnp.bfloat16) for value in floats],
            axis=1,
        )
        token_hidden = gelu(dot(token_one_t[...], normed), 0.5).astype(jnp.bfloat16)
        token_part = dot(token_two[...], token_hidden)
        mixed = jnp.concatenate(
            [
                floats[image] + token_part[:, image * model : (image + 1) * model]
                for image in range(group)
            ],
            axis=0,
        )
        second = layer_norm(mixed, gains[0, 1:2, :]).astype(jnp.bfloat16)

        hidden = gelu(dot(second, channel_one[...]), half).astype(jnp.bfloat16)
        total = (mixed + dot(hidden, channel_two[...])).astype(jnp.bfloat16)
        for image in range(group):
            rows = slice(image * patch_count, (image + 1) * patch_count)
            updated = jnp.where(active, total[rows], states[image])
            if finish:
                final = layer_norm(updated.astype(jnp.float32), final_gain[...])
                row = (first + image) % images * candidates + candidate
                pooled[pl.ds(row, 1), :] = jnp.mean(final, axis=0, keepdims=True)
            else:
                outbox[first + image] = updated
                hop(first + image).start()
        return carry

    loads[2].wait()
    loads[3].wait()
    @pl.when(section < last)
    def _():
        lax.fori_loop(0, units, functools.partial(step, 1, False), 0)

    @pl.when(section == last)
    def _():
        lax.fori_loop(0, candidates, functools.partial(step, images, True), 0)

    def tell(aa, ba):
        return pltpu.make_async_remote_copy(
            src_ref=share,
            dst_ref=landing.at[shard],
            send_sem=share_sem.at[aa * shards + ba],
            recv_sem=landing_sem.at[shard],
            device_id=(aa, ba),
            device_id_type=MESH,
        )

    def each_other(act):
        def visit(target, carry):
            aa, ba = target // shards, target % shards

            @pl.when(jnp.logical_or(aa != section, ba != shard))
            def _():
                act(tell(aa, ba))

            return carry

        lax.fori_loop(0, sections * shards, visit, 0)

    @pl.when(section == last)
    def _():
        head_load.wait()
        logits = lax.dot_general(
            pooled[...].astype(jnp.bfloat16),
            head[...],
            (((1,), (1,)), ((), ())),
            preferred_element_type=jnp.float32,
        )
        top = jnp.max(logits, axis=-1, keepdims=True)
        total = top + jnp.log(jnp.sum(jnp.exp(logits - top), axis=-1, keepdims=True))
        rows = lax.broadcasted_iota(jnp.int32, logits.shape, 0)
        classes = lax.broadcasted_iota(jnp.int32, logits.shape, 1)
        wanted = jnp.full(logits.shape, labels[0], jnp.int32)
        for image in range(1, images):
            wanted = jnp.where(rows >= image * candidates, labels[image], wanted)
        picked = jnp.sum(
            jnp.where(classes == wanted, logits, 0.0), axis=-1, keepdims=True
        )
        losses = total - picked
        summed = losses[:candidates]
        for image in range(1, images):
            summed = summed + losses[image * candidates : (image + 1) * candidates]
        lanes = out.shape[1]
        rows = lax.broadcasted_iota(jnp.int32, (candidates, lanes), 0)
        cols = lax.broadcasted_iota(jnp.int32, (candidates, lanes), 1)
        spread = jnp.broadcast_to(summed, (candidates, lanes))
        line = jnp.sum(jnp.where(rows == cols, spread, 0.0), axis=0, keepdims=True)
        share[...] = line
        landing[shard] = line
        each_other(lambda copy: copy.start())
        each_other(lambda copy: copy.wait_send())

    @pl.when(section < last)
    def _():
        def drain(unit, carry):
            hop(unit).wait_send()
            return carry

        lax.fori_loop(0, units, drain, 0)

    for origin in range(shards):

        @pl.when(jnp.logical_or(section < last, shard != origin))
        def _():
            pltpu.make_async_remote_copy(
                src_ref=share,
                dst_ref=landing.at[origin],
                send_sem=share_sem.at[0],
                recv_sem=landing_sem.at[origin],
                device_id=(last, origin),
                device_id_type=MESH,
            ).wait_recv()

    result = landing[0]
    for origin in range(1, shards):
        result = result + landing[origin]
    out[...] = result


def solution(mesh):
    sections, shards = mesh.shape["aa"], mesh.shape["ba"]

    def local(
        patches,
        token_first,
        token_second,
        channel_first,
        channel_second,
        gains,
        final_gain,
        head_weight,
        depths,
        widths,
        labels,
    ):
        images, patch_count, model = patches.shape
        candidates = depths.shape[0]
        units = candidates * images
        lanes = pl.cdiv(candidates, 128) * 128
        smem = pl.BlockSpec(memory_space=pltpu.SMEM)
        vmem = pl.BlockSpec(memory_space=pltpu.VMEM)
        hbm = pl.BlockSpec(memory_space=pl.ANY)
        line = pl.pallas_call(
            functools.partial(kernel, sections, shards),
            out_shape=jax.ShapeDtypeStruct((1, lanes), jnp.float32),
            in_specs=[smem] * 3 + [vmem] + [hbm] * 4 + [vmem] * 2 + [hbm],
            out_specs=vmem,
            scratch_shapes=[
                pltpu.VMEM((units, patch_count, model), jnp.bfloat16),
                pltpu.VMEM((units, patch_count, model), jnp.bfloat16),
                pltpu.VMEM(token_first.shape[1:], jnp.bfloat16),
                pltpu.VMEM(token_second.shape[1:], jnp.bfloat16),
                pltpu.VMEM(channel_first.shape[1:], jnp.bfloat16),
                pltpu.VMEM(channel_second.shape[1:], jnp.bfloat16),
                pltpu.VMEM(head_weight.shape[::-1], jnp.bfloat16),
                pltpu.VMEM((token_first.shape[2], patch_count), jnp.bfloat16),
                pltpu.VMEM((units, model), jnp.float32),
                pltpu.VMEM((1, lanes), jnp.float32),
                pltpu.VMEM((shards, 1, lanes), jnp.float32),
                pltpu.SemaphoreType.DMA((units,)),
                pltpu.SemaphoreType.DMA((units,)),
                pltpu.SemaphoreType.DMA((sections * shards,)),
                pltpu.SemaphoreType.DMA((shards,)),
                pltpu.SemaphoreType.DMA((5,)),
            ],
            compiler_params=pltpu.CompilerParams(
                collective_id=0, has_side_effects=True
            ),
        )(
            depths.T,
            widths.T,
            labels,
            patches,
            token_first,
            token_second,
            channel_first,
            channel_second,
            gains,
            final_gain[None, :],
            head_weight.T,
        )
        return line[0, :candidates]

    return jax.shard_map(
        local,
        mesh=mesh,
        in_specs=(
            P("ba", None, None),
            P("aa", None, None),
            P("aa", None, None),
            P("aa", None, None),
            P("aa", None, None),
            P("aa", None, None),
            P(),
            P(),
            P(),
            P(),
            P("ba"),
        ),
        out_specs=P(),
        check_vma=False,
    )
```
